1024 devices in a mesh: group: 64 (over y, z_hi, core), tensor: 16 (over z_lo, x).
Axes of the slice: x: 4, y: 8, z: 16 (z_hi: 4, z_lo: 4; z = z_hi * 4 + z_lo), core: 2. Of those that a mesh axis runs over, the one named last changes fastest.
Arguments:
- latents: bfloat16 [64, 256, 3072], P('group', 'tensor'), may hold values from -6 to 6
- stored_sample: bfloat16 [64, 256, 3072], P('group', 'tensor'), may hold values from -6 to 6
- timestep: int32 [64], P('group'), may hold values from 0 to 7
- owner_map: int32 [64], replicated, may hold values from 0 to 63, each once
- mod_table: float32 [8, 3, 3072], replicated, may hold values from -3 to 3
- qkv_weight: bfloat16 [3072, 6144], P('group', 'tensor'), may hold values from -0.5412659 to 0.5412659
- out_weight: bfloat16 [2048, 3072], P('tensor', 'group'), may hold values from -0.125 to 0.125
Outputs:
- mean_next: bfloat16 [64, 256, 3072], P('group', 'tensor')
- log_prob: float32 [64], P('group')
The draws below stay inside these ranges and needn't reach their ends.
Inputs may be any that keep to these rules, and one draw needn't show every extreme that they name: `owner_map`: each index of group holds exactly one slice.
All inputs are finite; a program needn't handle non-finite values.
Results may differ from the reference program's by a relative error of at most 0.0075.
Values may be sent and summed in bfloat16 or wider, within the bound.
No kernel may reach another device: no remote copies, remote signals or barrier semaphores. Data moves between devices by JAX's collectives and lax.ppermute only.
A program may use at most 32 MiB of HBM per device.

```python
import math
import jax
import jax.numpy as jnp
from jax import lax

D = 3072
HD = 128
HEADS = 16
SEQ = 256
STEPS = 8
BATCH = 64
N_GROUP = 64


def draw_qkv_weight(key, part):
    base = jax.random.normal(key, (D, HEADS, 3, HD), jnp.float32) * D ** (-0.5)
    base = jnp.clip(base, -6.0 * D ** (-0.5), 6.0 * D ** (-0.5))
    return base.reshape(D, HEADS * 3 * HD).astype(jnp.bfloat16)


def with_ends(entries, own_key, low, top_value):
    longest = entries.shape.index(max(entries.shape))
    spots = []
    for shift in (0, 1):
        where = [jax.random.randint(jax.random.fold_in(own_key, axis), (), 0, length) for axis, length in enumerate(entries.shape)]
        where[longest] = (where[longest] + shift) % entries.shape[longest]
        spots.append(tuple(where))
    return entries.at[spots[0]].set(low).at[spots[1]].set(top_value)


def levels(stream_key, dims, cuts, least, largest):
    loudness = 1.0
    for axis_at, blocks in cuts:
        steps = jax.random.uniform(jax.random.fold_in(jax.random.fold_in(stream_key, 6), axis_at), (blocks,), jnp.float32, least / len(cuts), largest / len(cuts))
        loudness = loudness * jnp.repeat(jnp.exp(steps), dims[axis_at] // blocks).reshape((-1,) + (1,) * (len(dims) - 1 - axis_at))
    return loudness


def scatter_about(own_key, extent, width, reach, shards=(), held_as=jnp.bfloat16):
    drawn = jax.random.normal(own_key, extent, jnp.float32) * width
    if len(shards) > 0:
        drawn = levels(own_key, extent, shards, -0.22, 0.18) * drawn
    return jnp.clip(drawn, min=-reach, max=reach).astype(held_as)


def setup_inputs(seed: int = 0) -> dict:
    keys = jax.random.split(jax.random.key(seed), 8)
    return {
        "latents": scatter_about(keys[0], (BATCH, SEQ, D), 1.0, 6.0, ((0, 64), (1, 16))),
        "stored_sample": scatter_about(keys[1], (BATCH, SEQ, D), 1.0, 6.0, ((0, 64), (1, 16))),
        "timestep": with_ends(jax.random.randint(keys[2], (BATCH,), 0, STEPS), jax.random.fold_in(keys[2], 1), 0, STEPS - 1).astype(jnp.int32),
        "owner_map": jax.random.permutation(keys[3], N_GROUP).astype(jnp.int32),
        "mod_table": scatter_about(keys[4], (STEPS, 3, D), 0.5, 3.0, (), jnp.float32),
        "qkv_weight": draw_qkv_weight(jax.random.fold_in(keys[7], 71), 0),
        "out_weight": scatter_about(keys[6], (HEADS * HD, D), (HEADS * HD) ** -0.5, 0.125, ((0, 16), (1, 64))),
    }


def reference(latents, stored_sample, timestep, owner_map, mod_table, qkv_weight, out_weight):
    slice_rows = D // N_GROUP
    qkv_true = qkv_weight.reshape(N_GROUP, slice_rows, HEADS * 3 * HD)[owner_map].reshape(D, HEADS * 3 * HD)
    out_true = out_weight.reshape(HEADS * HD, N_GROUP, slice_rows)[:, owner_map].reshape(HEADS * HD, D)
    out_heads = out_true.reshape(HEADS, HD, D)

    def one_sample(items):
        latent, stored, step_index = items
        modulation = mod_table[step_index]
        latent_f = latent.astype(jnp.float32)
        centred = latent_f - lax.optimization_barrier(jnp.mean(latent_f, axis=-1, keepdims=True))
        variance = lax.optimization_barrier(jnp.mean(centred * centred, axis=-1, keepdims=True))
        normed = centred * lax.rsqrt(variance + 1e-06)
        modulated = (normed * (1.0 + modulation[1]) + modulation[0]).astype(jnp.bfloat16)
        qkv = jnp.dot(modulated, qkv_true, preferred_element_type=jnp.float32).astype(jnp.bfloat16)
        qkv = qkv.reshape(SEQ, HEADS, 3, HD).transpose(1, 2, 0, 3)

        def one_head(parts):
            attention_scores = jnp.dot(parts[0], parts[1].T, preferred_element_type=jnp.float32) / math.sqrt(HD)
            attention_scores = attention_scores - lax.optimization_barrier(jnp.max(attention_scores, axis=-1, keepdims=True))
            expo = jnp.exp(attention_scores)
            attention_probabilities = (expo / lax.optimization_barrier(jnp.sum(expo, axis=-1, keepdims=True))).astype(jnp.bfloat16)
            return jnp.dot(attention_probabilities, parts[2], preferred_element_type=jnp.float32).astype(jnp.bfloat16)
        attended = lax.map(one_head, qkv)

        def add_head(total, pair):
            term = jnp.dot(pair[0], pair[1], preferred_element_type=jnp.float32).astype(jnp.bfloat16)
            term = lax.optimization_barrier(term)
            return (total + term.astype(jnp.float32), None)
        proj, unused = lax.scan(add_head, jnp.zeros((SEQ, D), jnp.float32), (attended, out_heads))
        hidden = latent_f + modulation[2] * proj
        time_float = step_index.astype(jnp.float32)
        step_size = (time_float + 1.0) / STEPS
        mean = latent_f - step_size * hidden
        noise_sigma_scale = 0.3 + 0.1 * time_float
        residual = stored.astype(jnp.float32) - mean
        log_prob = -jnp.sum(residual * residual) / (2.0 * noise_sigma_scale * noise_sigma_scale * SEQ * D) - jnp.log(noise_sigma_scale) - 0.5 * math.log(2.0 * math.pi)
        return (mean.astype(jnp.bfloat16), log_prob)
    return lax.map(one_sample, (latents, stored_sample, timestep))
```

```python
import functools
import math

import jax
import jax.numpy as jnp
from jax import lax
from jax.experimental import pallas as pl
from jax.experimental.pallas import tpu as pltpu
from jax.sharding import Mesh, PartitionSpec as P

GROUP = ("y", "zh", "core")
TENSOR = ("zl", "x")
NY, NZH, NCORE, NZL, NX = 8, 4, 2, 4, 4
NT = (((1,), (1,)), ((), ()))


def to_all(x, axis):
    copies = jnp.broadcast_to(x, (lax.axis_size(axis), *x.shape))
    return lax.all_to_all(copies, axis, split_axis=0, concat_axis=0, tiled=True)


def shifted(x, by):
    return lax.ppermute(x, "y", [(i, (i + by) % NY) for i in range(NY)])


def around_y(x):
    up = down = x
    found = [x]
    for step in range(NY // 2):
        up = shifted(up, 1)
        found.append(up)
        if step < NY // 2 - 1:
            down = shifted(down, -1)
            found.append(down)
    return jnp.concatenate(found, axis=0)


def norm_kernel(x_ref, mod_ref, o_ref):
    rows, width = x_ref.shape
    block = 32

    @pl.loop(0, rows // block)
    def _(i):
        here = pl.ds(pl.multiple_of(i * block, block), block)
        x = x_ref[here, :].astype(jnp.float32)
        centred = x - jnp.sum(x, axis=1, keepdims=True) / width
        variance = jnp.sum(centred * centred, axis=1, keepdims=True) / width
        normed = centred * lax.rsqrt(variance + 1e-06)
        o_ref[here, :] = (normed * (1.0 + mod_ref[1:2, :]) + mod_ref[0:1, :]).astype(jnp.bfloat16)


def normalised(tokens, mod):
    rows, width = tokens.shape
    vmem = pl.BlockSpec(memory_space=pltpu.VMEM)
    return pl.pallas_call(
        norm_kernel,
        out_shape=jax.ShapeDtypeStruct((rows, width), jnp.bfloat16),
        in_specs=[vmem, vmem],
        out_specs=vmem,
        compiler_params=pltpu.CompilerParams(vmem_limit_bytes=16 * 1024 * 1024),
        cost_estimate=pl.CostEstimate(
            flops=12 * rows * width, bytes_accessed=4 * rows * width, transcendentals=rows
        ),
    )(tokens, mod)


def head_kernel(at_ref, side_ref, x_ref, own_ref, other_ref, o_ref, w_ref):
    slices, rows = at_ref.shape[0], own_ref.shape[1]
    seq, width = x_ref.shape
    hd = own_ref.shape[2] // 4

    @pl.loop(0, slices)
    def _(s):
        here = pl.ds(pl.multiple_of(s * rows, rows), rows)

        @pl.when(side_ref[s] == 0)
        def _():
            w_ref[here, :] = own_ref[at_ref[s]]

        @pl.when(side_ref[s] != 0)
        def _():
            w_ref[here, :] = other_ref[at_ref[s]]

    qkv = jnp.dot(x_ref[...], w_ref[:, : 3 * hd], preferred_element_type=jnp.float32)
    qkv = qkv.astype(jnp.bfloat16)
    q, k, v = qkv[:, :hd], qkv[:, hd : 2 * hd], qkv[:, 2 * hd :]
    scores = lax.dot_general(q, k, NT, preferred_element_type=jnp.float32) / math.sqrt(hd)
    expo = jnp.exp(scores - jnp.max(scores, axis=1, keepdims=True))
    probs = (expo / jnp.sum(expo, axis=1, keepdims=True)).astype(jnp.bfloat16)
    attended = jnp.dot(probs, v, preferred_element_type=jnp.float32).astype(jnp.bfloat16)
    step = 512
    for at in range(0, width, step):
        w_out = w_ref[at : at + step, 3 * hd :]
        term = lax.dot_general(attended, w_out, NT, preferred_element_type=jnp.float32)
        term = term.astype(jnp.bfloat16).reshape(NZL, NX, seq // (NZL * NX), step)
        for x in range(NX):
            o_ref[x, :, :, at : at + step] = term[:, x]


def head_term(tokens, own, other, at, side):
    seq, width = tokens.shape
    smem = pl.BlockSpec(memory_space=pltpu.SMEM)
    vmem = pl.BlockSpec(memory_space=pltpu.VMEM)
    hd = own.shape[2] // 4
    return pl.pallas_call(
        head_kernel,
        out_shape=jax.ShapeDtypeStruct(
            (NX, NZL, seq // (NX * NZL), width), jnp.bfloat16
        ),
        in_specs=[smem, smem, vmem, vmem, vmem],
        out_specs=vmem,
        scratch_shapes=[pltpu.VMEM((width, own.shape[2]), jnp.bfloat16)],
        compiler_params=pltpu.CompilerParams(vmem_limit_bytes=48 * 1024 * 1024),
        cost_estimate=pl.CostEstimate(
            flops=8 * seq * width * hd, bytes_accessed=8 * seq * width, transcendentals=seq * seq
        ),
    )(at, side, tokens, own, other)


def shards(latents, stored_sample, timestep, owner_map, mod_table, qkv_weight, out_weight):
    samples, tok_local, width = latents.shape
    step_count = mod_table.shape[0]
    seq_len = tok_local * NZL * NX
    t = timestep[0]
    mod = lax.dynamic_index_in_dim(mod_table, t, 0, keepdims=False)

    weights = jnp.concatenate([qkv_weight, out_weight.T], axis=1)
    plane = lax.all_gather(weights, "zh")
    sent, plane = lax.optimization_barrier((latents[0], plane))
    tokens = to_all(sent, TENSOR).reshape(seq_len, width)
    own = around_y(plane)
    other = lax.ppermute(own, "core", [(0, 1), (1, 0)])

    far = (owner_map // (NZH * NCORE) - lax.axis_index("y")) % NY
    place = jnp.array([0, 2, 4, 6, 7, 5, 3, 1], jnp.int32)
    place_of = jnp.sum(
        jnp.where(far[:, None] == jnp.arange(NY)[None, :], place[None, :], 0), axis=1
    )
    at = (place_of * NZH + (owner_map // NCORE) % NZH).astype(jnp.int32)
    side = (owner_map % NCORE != lax.axis_index("core")).astype(jnp.int32)

    modulated = normalised(tokens, mod)
    terms = head_term(modulated, own, other, at, side)
    some = lax.all_to_all(terms, "x", split_axis=0, concat_axis=0, tiled=True)
    some = some.astype(jnp.float32).sum(axis=0).astype(jnp.bfloat16)
    parts = lax.all_to_all(some, "zl", split_axis=0, concat_axis=0, tiled=True)
    proj = parts.astype(jnp.float32).sum(axis=0)

    latent_f = latents[0].astype(jnp.float32)
    hidden = latent_f + mod[2:3] * proj
    time_float = t.astype(jnp.float32)
    step_size = (time_float + 1.0) / step_count
    mean = latent_f - step_size * hidden
    sigma = 0.3 + 0.1 * time_float
    residual = stored_sample[0].astype(jnp.float32) - mean
    total = to_all(jnp.sum(residual * residual), TENSOR).sum()
    log_prob = (
        -total / (2.0 * sigma * sigma * seq_len * width)
        - jnp.log(sigma)
        - 0.5 * math.log(2.0 * math.pi)
    )
    return (mean.astype(jnp.bfloat16)[None], log_prob[None])


def solution(mesh):
    fine = Mesh(mesh.devices.reshape(NY, NZH, NCORE, NZL, NX), GROUP + TENSOR)
    in_specs = (
        P(GROUP, TENSOR, None),
        P(GROUP, TENSOR, None),
        P(GROUP),
        P(),
        P(),
        P(GROUP, TENSOR),
        P(TENSOR, GROUP),
    )
    out_specs = (P(GROUP, TENSOR, None), P(GROUP))
    return jax.shard_map(shards, mesh=fine, in_specs=in_specs, out_specs=out_specs, check_vma=False)
```

```python
import math

import jax
import jax.numpy as jnp
from jax import lax
from jax.experimental import pallas as pl
from jax.experimental.pallas import tpu as pltpu
from jax.sharding import Mesh, PartitionSpec as P


GROUP = ("y", "zh", "core")
TENSOR = ("zl", "x")
NY, NZH, NCORE, NZL, NX = 8, 4, 2, 4, 4
NT = (((1,), (1,)), ((), ()))


def to_all(x, axis):
    copies = jnp.broadcast_to(x, (lax.axis_size(axis), *x.shape))
    return lax.all_to_all(copies, axis, split_axis=0, concat_axis=0, tiled=True)


def shifted(x, by):
    return lax.ppermute(x, "y", [(i, (i + by) % NY) for i in range(NY)])


def swapped(x):
    return lax.ppermute(x, "core", [(0, 1), (1, 0)])


PLACE = (0, 2, 6, 5, 3, 7, 4, 1)


def around_y(x):
    below = shifted(x, 1)
    above = shifted(x, -1)
    across = shifted(x, 4)
    near = jnp.concatenate([x, below, above, across], axis=0)
    up = shifted(jnp.concatenate([below, across], axis=0), 1)
    down = shifted(jnp.concatenate([above, across], axis=0), -1)
    return near, jnp.concatenate([up, down], axis=0)


def norm_kernel(x_ref, mod_ref, o_ref):
    rows, width = x_ref.shape
    block = 32

    @pl.loop(0, rows // block)
    def _(i):
        here = pl.ds(pl.multiple_of(i * block, block), block)
        x = x_ref[here, :].astype(jnp.float32)
        centred = x - jnp.sum(x, axis=1, keepdims=True) / width
        variance = jnp.sum(centred * centred, axis=1, keepdims=True) / width
        normed = centred * lax.rsqrt(variance + 1e-06)
        o_ref[here, :] = (normed * (1.0 + mod_ref[1:2, :]) + mod_ref[0:1, :]).astype(jnp.bfloat16)


def normalised(tokens, mod):
    rows, width = tokens.shape
    vmem = pl.BlockSpec(memory_space=pltpu.VMEM)
    return pl.pallas_call(
        norm_kernel,
        out_shape=jax.ShapeDtypeStruct((rows, width), jnp.bfloat16),
        in_specs=[vmem, vmem],
        out_specs=vmem,
        compiler_params=pltpu.CompilerParams(vmem_limit_bytes=16 * 1024 * 1024),
        cost_estimate=pl.CostEstimate(
            flops=12 * rows * width, bytes_accessed=4 * rows * width, transcendentals=rows
        ),
    )(tokens, mod)


def head_kernel(at_ref, x_ref, own0, own1, other0, other1, o_ref, w_ref):
    slices, (count, rows, columns) = at_ref.shape[0], own0.shape
    width = x_ref.shape[1]
    hd = columns // 4

    @pl.loop(0, slices)
    def _(s):
        here = pl.ds(pl.multiple_of(s * rows, rows), rows)
        at = at_ref[s]
        for part, ref in enumerate((own0, own1, other0, other1)):

            @pl.when(at // count == part)
            def _():
                w_ref[here, :] = ref[at % count]

    qkv = jnp.dot(x_ref[...], w_ref[:, : 3 * hd], preferred_element_type=jnp.float32)
    qkv = qkv.astype(jnp.bfloat16)
    q, k, v = qkv[:, :hd], qkv[:, hd : 2 * hd], qkv[:, 2 * hd :]
    scores = lax.dot_general(q, k, NT, preferred_element_type=jnp.float32) / math.sqrt(hd)
    expo = jnp.exp(scores - jnp.max(scores, axis=1, keepdims=True))
    probs = (expo / jnp.sum(expo, axis=1, keepdims=True)).astype(jnp.bfloat16)
    attended = jnp.dot(probs, v, preferred_element_type=jnp.float32).astype(jnp.bfloat16)
    step = 512
    for c in range(0, width, step):
        w_out = w_ref[c : c + step, 3 * hd :]
        term = lax.dot_general(attended, w_out, NT, preferred_element_type=jnp.float32)
        o_ref[:, c : c + step] = term.astype(jnp.bfloat16)


def head_term(tokens, pieces, at):
    seq, width = tokens.shape
    smem = pl.BlockSpec(memory_space=pltpu.SMEM)
    vmem = pl.BlockSpec(memory_space=pltpu.VMEM)
    columns = pieces[0].shape[2]
    return pl.pallas_call(
        head_kernel,
        out_shape=jax.ShapeDtypeStruct((seq, width), jnp.bfloat16),
        in_specs=[smem] + [vmem] * 5,
        out_specs=vmem,
        scratch_shapes=[pltpu.VMEM((width, columns), jnp.bfloat16)],
        compiler_params=pltpu.CompilerParams(vmem_limit_bytes=40 * 1024 * 1024),
        cost_estimate=pl.CostEstimate(
            flops=2 * seq * width * columns,
            bytes_accessed=8 * seq * width,
            transcendentals=seq * seq,
        ),
    )(at, tokens, *pieces)


def mean_kernel(dt_ref, parts_ref, latent_ref, stored_ref, gate_ref, mean_ref, sum_ref):
    dt = dt_ref[0]
    devices, rows, width = parts_ref.shape
    step = 512
    squares = jnp.zeros((rows, step), jnp.float32)
    for c in range(0, width, step):
        here = slice(c, c + step)
        proj = parts_ref[0, :, here].astype(jnp.float32)
        for k in range(1, devices):
            proj = proj + parts_ref[k, :, here].astype(jnp.float32)
        latent = latent_ref[:, here].astype(jnp.float32)
        mean = latent - dt * (latent + gate_ref[:, here] * proj)
        mean_ref[:, here] = mean.astype(jnp.bfloat16)
        residual = stored_ref[:, here].astype(jnp.float32) - mean
        squares = squares + residual * residual
    total = jnp.sum(squares, axis=(0, 1), keepdims=True)
    sum_ref[...] = jnp.broadcast_to(total[None], sum_ref.shape)


def mean_and_squares(dt, parts, latent, stored, gate):
    devices, rows, width = parts.shape
    vmem = pl.BlockSpec(memory_space=pltpu.VMEM)
    return pl.pallas_call(
        mean_kernel,
        out_shape=(
            jax.ShapeDtypeStruct((rows, width), jnp.bfloat16),
            jax.ShapeDtypeStruct((devices, 1, 128), jnp.float32),
        ),
        in_specs=[pl.BlockSpec(memory_space=pltpu.SMEM)] + [vmem] * 4,
        out_specs=(vmem, vmem),
        compiler_params=pltpu.CompilerParams(vmem_limit_bytes=16 * 1024 * 1024),
        cost_estimate=pl.CostEstimate(
            flops=30 * rows * width, bytes_accessed=40 * rows * width, transcendentals=0
        ),
    )(dt, parts, latent, stored, gate)


def one_device(latents, stored_sample, timestep, owner_map, mod_table, qkv_weight, out_weight):
    _, tok_local, width = latents.shape
    step_count = mod_table.shape[0]
    seq_len = tok_local * NZL * NX
    t = timestep[0]
    time_float = t.astype(jnp.float32)
    mod = lax.dynamic_index_in_dim(mod_table, t, 0, keepdims=False)

    weights = jnp.concatenate([qkv_weight, out_weight.T], axis=1)
    plane = lax.all_gather(weights, "zh", tiled=False)
    sent, plane = lax.optimization_barrier((latents[0], plane))
    tokens = to_all(sent, TENSOR).reshape(seq_len, width)
    near, far = around_y(plane)
    pieces = (near, far, swapped(near), swapped(far))

    ahead = (owner_map // (NZH * NCORE) - lax.axis_index("y")) % NY
    place = jnp.zeros_like(ahead)
    for distance, where in enumerate(PLACE):
        place = jnp.where(ahead == distance, where, place)
    side = (owner_map % NCORE != lax.axis_index("core")).astype(jnp.int32)
    at = ((side * NY + place) * NZH + (owner_map // NCORE) % NZH).astype(jnp.int32)

    modulated = normalised(tokens, mod)
    terms = head_term(modulated, pieces, at)
    parts = lax.all_to_all(
        terms.reshape(NZL * NX, tok_local, width), TENSOR, split_axis=0, concat_axis=0, tiled=True
    )
    dt = (timestep.astype(jnp.float32) + 1.0) / step_count
    mean, squares = mean_and_squares(dt, parts, latents[0], stored_sample[0], mod[2:3])
    squares = lax.all_to_all(squares, TENSOR, split_axis=0, concat_axis=0, tiled=True)
    total = jnp.sum(squares[:, :, :1])
    sigma = 0.3 + 0.1 * time_float
    log_prob = (
        -total / (2.0 * sigma * sigma * seq_len * width)
        - jnp.log(sigma)
        - 0.5 * math.log(2.0 * math.pi)
    )
    return (mean[None], log_prob[None])


def solution(mesh):
    fine = Mesh(mesh.devices.reshape(NY, NZH, NCORE, NZL, NX), GROUP + TENSOR)
    in_specs = (
        P(GROUP, TENSOR, None),
        P(GROUP, TENSOR, None),
        P(GROUP),
        P(),
        P(),
        P(GROUP, TENSOR),
        P(TENSOR, GROUP),
    )
    out_specs = (P(GROUP, TENSOR, None), P(GROUP))
    return jax.shard_map(one_device, mesh=fine, in_specs=in_specs, out_specs=out_specs, check_vma=False)
```

```python
import math

import jax
import jax.numpy as jnp
from jax import lax
from jax.experimental import pallas as pl
from jax.experimental.pallas import tpu as pltpu
from jax.sharding import Mesh, PartitionSpec as P

GROUP = ("y", "zh", "core")
TENSOR = ("zl", "x")
NY, NZH, NCORE, NZL, NX = 8, 4, 2, 4, 4
NT = (((1,), (1,)), ((), ()))


def to_all(x, axis):
    copies = jnp.broadcast_to(x, (lax.axis_size(axis), *x.shape))
    return lax.all_to_all(copies, axis, split_axis=0, concat_axis=0, tiled=True)


def shifted(x, by, name):
    with jax.named_scope(name):
        return lax.ppermute(x, "y", [(i, (i + by) % NY) for i in range(NY)])


def swapped(x):
    return lax.ppermute(x, "core", [(0, 1), (1, 0)])


PLACE = (0, 2, 6, 5, 3, 7, 4, 1)


def around_y(x):
    below = shifted(x, 1, "w_up")
    above = shifted(x, -1, "w_down")
    across = shifted(x, 4, "w_four")
    near = jnp.concatenate([x, below, above, across], axis=0)
    up = shifted(jnp.concatenate([below, across], axis=0), 1, "w_up2")
    down = shifted(jnp.concatenate([above, across], axis=0), -1, "w_down2")
    return near, jnp.concatenate([up, down], axis=0)


def norm_kernel(x_ref, mod_ref, o_ref):
    rows, width = x_ref.shape
    block = 32

    @pl.loop(0, rows // block)
    def _(i):
        here = pl.ds(pl.multiple_of(i * block, block), block)
        x = x_ref[here, :].astype(jnp.float32)
        centred = x - jnp.sum(x, axis=1, keepdims=True) / width
        variance = jnp.sum(centred * centred, axis=1, keepdims=True) / width
        normed = centred * lax.rsqrt(variance + 1e-06)
        o_ref[here, :] = (normed * (1.0 + mod_ref[1:2, :]) + mod_ref[0:1, :]).astype(jnp.bfloat16)


def normalised(tokens, mod):
    rows, width = tokens.shape
    vmem = pl.BlockSpec(memory_space=pltpu.VMEM)
    return pl.pallas_call(
        norm_kernel,
        out_shape=jax.ShapeDtypeStruct((rows, width), jnp.bfloat16),
        in_specs=[vmem, vmem],
        out_specs=vmem,
        compiler_params=pltpu.CompilerParams(vmem_limit_bytes=16 * 1024 * 1024),
        cost_estimate=pl.CostEstimate(
            flops=12 * rows * width, bytes_accessed=4 * rows * width, transcendentals=rows
        ),
    )(tokens, mod)


def head_kernel(to_ref, x_ref, own0, own1, other0, other1, o_ref, w_ref):
    count, rows, columns = own0.shape
    width = x_ref.shape[1]
    hd = columns // 4
    for part, ref in enumerate((own0, own1, other0, other1)):
        for k in range(count):
            first = pl.multiple_of(to_ref[part * count + k] * rows, rows)
            w_ref[pl.ds(first, rows), :] = ref[k]

    qkv = jnp.dot(x_ref[...], w_ref[:, : 3 * hd], preferred_element_type=jnp.float32)
    qkv = qkv.astype(jnp.bfloat16)
    q, k, v = qkv[:, :hd], qkv[:, hd : 2 * hd], qkv[:, 2 * hd :]
    scores = lax.dot_general(q, k, NT, preferred_element_type=jnp.float32) / math.sqrt(hd)
    expo = jnp.exp(scores - jnp.max(scores, axis=1, keepdims=True))
    probs = (expo / jnp.sum(expo, axis=1, keepdims=True)).astype(jnp.bfloat16)
    attended = jnp.dot(probs, v, preferred_element_type=jnp.float32).astype(jnp.bfloat16)
    step = 512
    for c in range(0, width, step):
        w_out = w_ref[c : c + step, 3 * hd :]
        term = lax.dot_general(attended, w_out, NT, preferred_element_type=jnp.float32)
        o_ref[:, c : c + step] = term.astype(jnp.bfloat16)


def head_term(tokens, pieces, slots):
    seq, width = tokens.shape
    smem = pl.BlockSpec(memory_space=pltpu.SMEM)
    vmem = pl.BlockSpec(memory_space=pltpu.VMEM)
    columns = pieces[0].shape[2]
    return pl.pallas_call(
        head_kernel,
        out_shape=jax.ShapeDtypeStruct((seq, width), jnp.bfloat16),
        in_specs=[smem] + [vmem] * 5,
        out_specs=vmem,
        scratch_shapes=[pltpu.VMEM((width, columns), jnp.bfloat16)],
        compiler_params=pltpu.CompilerParams(vmem_limit_bytes=40 * 1024 * 1024),
        cost_estimate=pl.CostEstimate(
            flops=2 * seq * width * columns,
            bytes_accessed=8 * seq * width,
            transcendentals=seq * seq,
        ),
    )(slots, tokens, *pieces)


def mean_kernel(dt_ref, parts_ref, latent_ref, stored_ref, gate_ref, mean_ref, sum_ref):
    dt = dt_ref[0]
    devices, rows, width = parts_ref.shape
    step = 512
    squares = jnp.zeros((rows, step), jnp.float32)
    for c in range(0, width, step):
        here = slice(c, c + step)
        proj = parts_ref[0, :, here].astype(jnp.float32)
        for k in range(1, devices):
            proj = proj + parts_ref[k, :, here].astype(jnp.float32)
        latent = latent_ref[:, here].astype(jnp.float32)
        mean = latent - dt * (latent + gate_ref[:, here] * proj)
        mean_ref[:, here] = mean.astype(jnp.bfloat16)
        residual = stored_ref[:, here].astype(jnp.float32) - mean
        squares = squares + residual * residual
    total = jnp.sum(squares, axis=(0, 1), keepdims=True)
    sum_ref[...] = jnp.broadcast_to(total[None], sum_ref.shape)


def mean_and_squares(dt, parts, latent, stored, gate):
    devices, rows, width = parts.shape
    vmem = pl.BlockSpec(memory_space=pltpu.VMEM)
    return pl.pallas_call(
        mean_kernel,
        out_shape=(
            jax.ShapeDtypeStruct((rows, width), jnp.bfloat16),
            jax.ShapeDtypeStruct((devices, 1, 128), jnp.float32),
        ),
        in_specs=[pl.BlockSpec(memory_space=pltpu.SMEM)] + [vmem] * 4,
        out_specs=(vmem, vmem),
        compiler_params=pltpu.CompilerParams(vmem_limit_bytes=16 * 1024 * 1024),
        cost_estimate=pl.CostEstimate(
            flops=30 * rows * width, bytes_accessed=40 * rows * width, transcendentals=0
        ),
    )(dt, parts, latent, stored, gate)


def shards(latents, stored_sample, timestep, owner_map, mod_table, qkv_weight, out_weight):
    samples, tok_local, width = latents.shape
    step_count = mod_table.shape[0]
    seq_len = tok_local * NZL * NX
    t = timestep[0]
    time_float = t.astype(jnp.float32)
    mod = lax.dynamic_index_in_dim(mod_table, t, 0, keepdims=False)

    sigma = 0.3 + 0.1 * time_float
    dt = (timestep.astype(jnp.float32) + 1.0) / step_count
    spread = 2.0 * sigma * sigma * seq_len * width
    offset = jnp.log(sigma) + 0.5 * math.log(2.0 * math.pi)

    weights = jnp.concatenate([qkv_weight, out_weight.T], axis=1)
    plane = lax.all_gather(weights, "zh", tiled=False)
    sent, plane = lax.optimization_barrier((latents[0], plane))
    tokens = to_all(sent, TENSOR).reshape(seq_len, width)
    near, far = around_y(plane)
    pieces = (near, far, swapped(near), swapped(far))

    ahead = (owner_map // (NZH * NCORE) - lax.axis_index("y")) % NY
    place = jnp.zeros_like(ahead)
    for distance, where in enumerate(PLACE):
        place = jnp.where(ahead == distance, where, place)
    side = (owner_map % NCORE != lax.axis_index("core")).astype(jnp.int32)
    at = (side * NY + place) * NZH + (owner_map // NCORE) % NZH
    slices = jnp.arange(at.shape[0], dtype=jnp.int32)
    slots = jnp.sum(jnp.where(at[None, :] == slices[:, None], slices[None, :], 0), axis=1)

    modulated = normalised(tokens, mod)
    terms = head_term(modulated, pieces, slots)
    terms, latent, stored, gate, dt, spread, offset = lax.optimization_barrier(
        (terms, latents[0], stored_sample[0], mod[2:3], dt, spread, offset)
    )
    parts = lax.all_to_all(
        terms.reshape(NZL * NX, tok_local, width), TENSOR, split_axis=0, concat_axis=0, tiled=True
    )
    mean, squares = mean_and_squares(dt, parts, latent, stored, gate)
    mean, squares = lax.optimization_barrier((mean, squares))
    squares = lax.all_to_all(squares, TENSOR, split_axis=0, concat_axis=0, tiled=True)
    log_prob = -jnp.sum(squares[:, :, :1]) / spread - offset
    return (mean[None], log_prob[None])


def solution(mesh):
    fine = Mesh(mesh.devices.reshape(NY, NZH, NCORE, NZL, NX), GROUP + TENSOR)
    in_specs = (
        P(GROUP, TENSOR, None),
        P(GROUP, TENSOR, None),
        P(GROUP),
        P(),
        P(),
        P(GROUP, TENSOR),
        P(TENSOR, GROUP),
    )
    out_specs = (P(GROUP, TENSOR, None), P(GROUP))
    return jax.shard_map(shards, mesh=fine, in_specs=in_specs, out_specs=out_specs, check_vma=False)
```

```python
import math

import jax
import jax.numpy as jnp
from jax import lax
from jax.experimental import pallas as pl
from jax.experimental.pallas import tpu as pltpu
from jax.sharding import Mesh, PartitionSpec as P

GROUP = ("y", "zh", "core")
TENSOR = ("zl", "x")
NY, NZH, NCORE, NZL, NX = 8, 4, 2, 4, 4
NT = (((1,), (1,)), ((), ()))


def to_all(x, axis):
    copies = jnp.broadcast_to(x, (lax.axis_size(axis), *x.shape))
    return lax.all_to_all(copies, axis, split_axis=0, concat_axis=0, tiled=True)


def shifted(x, by, name):
    with jax.named_scope(name):
        return lax.ppermute(x, "y", [(i, (i + by) % NY) for i in range(NY)])


def swapped(x):
    return lax.ppermute(x, "core", [(0, 1), (1, 0)])


PLACE = (0, 2, 6, 5, 3, 7, 4, 1)


def around_y(x):
    below = shifted(x, 1, "w_up")
    above = shifted(x, -1, "w_down")
    across = shifted(x, 4, "w_four")
    near = jnp.concatenate([x, below, above, across], axis=0)
    up = shifted(jnp.concatenate([below, across], axis=0), 1, "w_up2")
    down = shifted(jnp.concatenate([above, across], axis=0), -1, "w_down2")
    return near, jnp.concatenate([up, down], axis=0)


def norm_kernel(x_ref, mod_ref, o_ref):
    rows, width = x_ref.shape
    block = 32

    @pl.loop(0, rows // block)
    def _(i):
        here = pl.ds(pl.multiple_of(i * block, block), block)
        x = x_ref[here, :].astype(jnp.float32)
        centred = x - jnp.sum(x, axis=1, keepdims=True) / width
        variance = jnp.sum(centred * centred, axis=1, keepdims=True) / width
        normed = centred * lax.rsqrt(variance + 1e-06)
        o_ref[here, :] = (normed * (1.0 + mod_ref[1:2, :]) + mod_ref[0:1, :]).astype(jnp.bfloat16)


def normalised(tokens, mod):
    rows, width = tokens.shape
    vmem = pl.BlockSpec(memory_space=pltpu.VMEM)
    return pl.pallas_call(
        norm_kernel,
        out_shape=jax.ShapeDtypeStruct((rows, width), jnp.bfloat16),
        in_specs=[vmem, vmem],
        out_specs=vmem,
        compiler_params=pltpu.CompilerParams(vmem_limit_bytes=16 * 1024 * 1024),
        cost_estimate=pl.CostEstimate(
            flops=12 * rows * width, bytes_accessed=4 * rows * width, transcendentals=rows
        ),
    )(tokens, mod)


def head_kernel(to_ref, row_ref, x_ref, own0, own1, other0, other1, *rest):
    outs, (w_ref, a_ref) = rest[:NX], rest[NX:]
    count, rows, columns = own0.shape
    width = x_ref.shape[1]
    hd = columns // 4
    for part, ref in enumerate((own0, own1, other0, other1)):
        for k in range(count):
            first = pl.multiple_of(to_ref[part * count + k] * rows, rows)
            w_ref[pl.ds(first, rows), :] = ref[k]

    qkv = jnp.dot(x_ref[...], w_ref[:, : 3 * hd], preferred_element_type=jnp.float32)
    qkv = qkv.astype(jnp.bfloat16)
    q, k, v = qkv[:, :hd], qkv[:, hd : 2 * hd], qkv[:, 2 * hd :]
    scores = lax.dot_general(q, k, NT, preferred_element_type=jnp.float32) / math.sqrt(hd)
    expo = jnp.exp(scores - jnp.max(scores, axis=1, keepdims=True))
    probs = (expo / jnp.sum(expo, axis=1, keepdims=True)).astype(jnp.bfloat16)
    attended = jnp.dot(probs, v, preferred_element_type=jnp.float32)
    a_ref[...] = attended.astype(jnp.bfloat16)
    blocks = row_ref.shape[0]
    tok = a_ref.shape[0] // blocks
    ordered = jnp.concatenate(
        [a_ref[pl.ds(pl.multiple_of(row_ref[i], tok), tok), :] for i in range(blocks)], axis=0
    )
    step = 512
    part = ordered.shape[0] // NX
    for c in range(0, width, step):
        w_out = w_ref[c : c + step, 3 * hd :]
        term = lax.dot_general(ordered, w_out, NT, preferred_element_type=jnp.float32)
        term = term.astype(jnp.bfloat16)
        for r, o_ref in enumerate(outs):
            o_ref[:, c : c + step] = term[r * part : (r + 1) * part]


def head_term(tokens, pieces, slots, first_rows):
    seq, width = tokens.shape
    smem = pl.BlockSpec(memory_space=pltpu.SMEM)
    vmem = pl.BlockSpec(memory_space=pltpu.VMEM)
    columns = pieces[0].shape[2]
    return pl.pallas_call(
        head_kernel,
        out_shape=[jax.ShapeDtypeStruct((seq // NX, width), jnp.bfloat16)] * NX,
        in_specs=[smem] * 2 + [vmem] * 5,
        out_specs=[vmem] * NX,
        scratch_shapes=[
            pltpu.VMEM((width, columns), jnp.bfloat16),
            pltpu.VMEM((seq, columns // 4), jnp.bfloat16),
        ],
        compiler_params=pltpu.CompilerParams(vmem_limit_bytes=40 * 1024 * 1024),
        cost_estimate=pl.CostEstimate(
            flops=2 * seq * width * columns,
            bytes_accessed=8 * seq * width,
            transcendentals=seq * seq,
        ),
    )(slots, first_rows, tokens, *pieces)


def sum_kernel(*refs):
    ins, outs = refs[:NX], refs[NX:]
    rows = outs[0].shape[0]
    step = 1024
    for k, o_ref in enumerate(outs):
        for c in range(0, o_ref.shape[1], step):
            here = (slice(k * rows, (k + 1) * rows), slice(c, c + step))
            total = ins[0][here].astype(jnp.float32)
            for ref in ins[1:]:
                total = total + ref[here].astype(jnp.float32)
            o_ref[:, c : c + step] = total.astype(o_ref.dtype)


def summed(blocks):
    rows, width = blocks[0].shape
    vmem = pl.BlockSpec(memory_space=pltpu.VMEM)
    shape = (rows // NZL, width)
    return pl.pallas_call(
        sum_kernel,
        out_shape=[jax.ShapeDtypeStruct(shape, jnp.float32)]
        + [jax.ShapeDtypeStruct(shape, jnp.bfloat16)] * (NZL - 1),
        in_specs=[vmem] * NX,
        out_specs=[vmem] * NZL,
        compiler_params=pltpu.CompilerParams(vmem_limit_bytes=16 * 1024 * 1024),
        cost_estimate=pl.CostEstimate(
            flops=4 * rows * width, bytes_accessed=10 * rows * width, transcendentals=0
        ),
    )(*blocks)


def mean_kernel(dt_ref, p0, p1, p2, p3, latent_ref, stored_ref, gate_ref, mean_ref, sum_ref):
    dt = dt_ref[0]
    rows, width = p0.shape
    step = 512
    squares = jnp.zeros((rows, step), jnp.float32)
    for c in range(0, width, step):
        here = slice(c, c + step)
        proj = p0[:, here]
        for ref in (p1, p2, p3):
            proj = proj + ref[:, here].astype(jnp.float32)
        latent = latent_ref[:, here].astype(jnp.float32)
        mean = latent - dt * (latent + gate_ref[:, here] * proj)
        mean_ref[:, here] = mean.astype(jnp.bfloat16)
        residual = stored_ref[:, here].astype(jnp.float32) - mean
        squares = squares + residual * residual
    total = jnp.sum(squares, axis=(0, 1), keepdims=True)
    sum_ref[...] = jnp.broadcast_to(total[None], sum_ref.shape)


def mean_and_squares(dt, parts, latent, stored, gate):
    rows, width = latent.shape
    vmem = pl.BlockSpec(memory_space=pltpu.VMEM)
    return pl.pallas_call(
        mean_kernel,
        out_shape=(
            jax.ShapeDtypeStruct((rows, width), jnp.bfloat16),
            jax.ShapeDtypeStruct((NZL * NX, 1, 128), jnp.float32),
        ),
        in_specs=[pl.BlockSpec(memory_space=pltpu.SMEM)] + [vmem] * 7,
        out_specs=(vmem, vmem),
        compiler_params=pltpu.CompilerParams(vmem_limit_bytes=16 * 1024 * 1024),
        cost_estimate=pl.CostEstimate(
            flops=16 * rows * width, bytes_accessed=16 * rows * width, transcendentals=0
        ),
    )(dt, *parts, latent, stored, gate)


def shards(latents, stored_sample, timestep, owner_map, mod_table, qkv_weight, out_weight):
    samples, tok_local, width = latents.shape
    step_count = mod_table.shape[0]
    seq_len = tok_local * NZL * NX
    t = timestep[0]
    time_float = t.astype(jnp.float32)
    mod = lax.dynamic_index_in_dim(mod_table, t, 0, keepdims=False)

    sigma = 0.3 + 0.1 * time_float
    dt = (timestep.astype(jnp.float32) + 1.0) / step_count
    spread = 2.0 * sigma * sigma * seq_len * width
    offset = jnp.log(sigma) + 0.5 * math.log(2.0 * math.pi)

    weights = jnp.concatenate([qkv_weight, out_weight.T], axis=1)
    plane = lax.all_gather(weights, "zh", tiled=False)
    sent, plane = lax.optimization_barrier((latents[0], plane))
    tokens = to_all(sent, TENSOR).reshape(seq_len, width)
    near, far = around_y(plane)
    pieces = (near, far, swapped(near), swapped(far))

    ahead = (owner_map // (NZH * NCORE) - lax.axis_index("y")) % NY
    place = jnp.zeros_like(ahead)
    for distance, where in enumerate(PLACE):
        place = jnp.where(ahead == distance, where, place)
    side = (owner_map % NCORE != lax.axis_index("core")).astype(jnp.int32)
    at = (side * NY + place) * NZH + (owner_map // NCORE) % NZH
    slices = jnp.arange(at.shape[0], dtype=jnp.int32)
    slots = jnp.sum(jnp.where(at[None, :] == slices[:, None], slices[None, :], 0), axis=1)

    turn = jnp.arange(NX * NZL, dtype=jnp.int32)
    to_x = (lax.axis_index("x") + turn // NZL) % NX
    to_z = lax.axis_index("zl") ^ (turn % NZL)
    first_rows = ((to_z * NX + to_x) * tok_local).astype(jnp.int32)

    modulated = normalised(tokens, mod)
    terms = head_term(modulated, pieces, slots, first_rows)
    by_x = [terms[0]] + [
        lax.ppermute(terms[r], "x", [(i, (i + r) % NX) for i in range(NX)]) for r in (2, 1, 3)
    ]
    some = summed(by_x)
    by_z = [some[0]] + [
        lax.ppermute(some[k], "zl", [(i, i ^ k) for i in range(NZL)]) for k in (2, 3, 1)
    ]
    mean, squares = mean_and_squares(dt, by_z, latents[0], stored_sample[0], mod[2:3])
    mean, squares, spread, offset = lax.optimization_barrier((mean, squares, spread, offset))
    squares = lax.all_to_all(squares, TENSOR, split_axis=0, concat_axis=0, tiled=True)
    log_prob = -jnp.sum(squares[:, :, :1]) / spread - offset
    return (mean[None], log_prob[None])


def solution(mesh):
    fine = Mesh(mesh.devices.reshape(NY, NZH, NCORE, NZL, NX), GROUP + TENSOR)
    in_specs = (
        P(GROUP, TENSOR, None),
        P(GROUP, TENSOR, None),
        P(GROUP),
        P(),
        P(),
        P(GROUP, TENSOR),
        P(TENSOR, GROUP),
    )
    out_specs = (P(GROUP, TENSOR, None), P(GROUP))
    return jax.shard_map(shards, mesh=fine, in_specs=in_specs, out_specs=out_specs, check_vma=False)
```

```python
import math

import jax
import jax.numpy as jnp
from jax import lax
from jax.experimental import pallas as pl
from jax.experimental.pallas import tpu as pltpu
from jax.sharding import Mesh, PartitionSpec as P


GROUP = ("y", "zh", "core")
TENSOR = ("zl", "x")
NY, NZH, NCORE, NZL, NX = 8, 4, 2, 4, 4
NT = (((1,), (1,)), ((), ()))


def shifted(x, by):
    return lax.ppermute(x, "y", [(i, (i + by) % NY) for i in range(NY)])


def swapped(x):
    return lax.ppermute(x, "core", [(0, 1), (1, 0)])


PLACE = (0, 2, 6, 5, 3, 7, 4, 1)


def around_y(x):
    below = shifted(x, 1)
    above = shifted(x, -1)
    across = shifted(x, 4)
    near = jnp.concatenate([x, below, above, across], axis=0)
    up = shifted(jnp.concatenate([below, across], axis=0), 1)
    down = shifted(jnp.concatenate([above, across], axis=0), -1)
    return near, jnp.concatenate([up, down], axis=0)


def norm_kernel(t_ref, x_ref, table_ref, o_ref):
    t = t_ref[0]
    x = x_ref[...].astype(jnp.float32)
    width = x.shape[1]
    centred = x - jnp.sum(x, axis=1, keepdims=True) / width
    variance = jnp.sum(centred * centred, axis=1, keepdims=True) / width
    normed = centred * lax.rsqrt(variance + 1e-06)
    shift, scale = table_ref[0, pl.ds(t, 1), :], table_ref[1, pl.ds(t, 1), :]
    modulated = (normed * (1.0 + scale) + shift).astype(jnp.bfloat16)
    for i in range(o_ref.shape[0]):
        o_ref[i] = modulated


def normalised_copies(t, tokens, table, copies):
    rows, width = tokens.shape
    vmem = pl.BlockSpec(memory_space=pltpu.VMEM)
    return pl.pallas_call(
        norm_kernel,
        out_shape=jax.ShapeDtypeStruct((copies, rows, width), jnp.bfloat16),
        in_specs=[pl.BlockSpec(memory_space=pltpu.SMEM), vmem, vmem],
        out_specs=vmem,
        compiler_params=pltpu.CompilerParams(vmem_limit_bytes=16 * 1024 * 1024),
        cost_estimate=pl.CostEstimate(
            flops=12 * rows * width, bytes_accessed=40 * rows * width, transcendentals=rows
        ),
    )(t, tokens, table)


def head_kernel(to_ref, row_ref, x_ref, own0, own1, other0, other1, *rest):
    outs, (w_ref, a_ref) = rest[:NX], rest[NX:]
    count, rows, columns = own0.shape
    width = x_ref.shape[1]
    hd = columns // 4
    for part, ref in enumerate((own0, own1, other0, other1)):
        for k in range(count):
            first = pl.multiple_of(to_ref[part * count + k] * rows, rows)
            w_ref[pl.ds(first, rows), :] = ref[k]

    qkv = jnp.dot(x_ref[...], w_ref[:, : 3 * hd], preferred_element_type=jnp.float32)
    qkv = qkv.astype(jnp.bfloat16)
    q, k, v = qkv[:, :hd], qkv[:, hd : 2 * hd], qkv[:, 2 * hd :]
    scores = lax.dot_general(q, k, NT, preferred_element_type=jnp.float32) / math.sqrt(hd)
    expo = jnp.exp(scores - jnp.max(scores, axis=1, keepdims=True))
    probs = (expo / jnp.sum(expo, axis=1, keepdims=True)).astype(jnp.bfloat16)
    attended = jnp.dot(probs, v, preferred_element_type=jnp.float32)
    a_ref[...] = attended.astype(jnp.bfloat16)
    blocks = row_ref.shape[0]
    tok = a_ref.shape[0] // blocks
    ordered = jnp.concatenate(
        [a_ref[pl.ds(pl.multiple_of(row_ref[i], tok), tok), :] for i in range(blocks)], axis=0
    )
    step = 512
    part = ordered.shape[0] // NX
    for c in range(0, width, step):
        w_out = w_ref[c : c + step, 3 * hd :]
        term = lax.dot_general(ordered, w_out, NT, preferred_element_type=jnp.float32)
        term = term.astype(jnp.bfloat16)
        for r, o_ref in enumerate(outs):
            o_ref[:, c : c + step] = term[r * part : (r + 1) * part]


def head_term(tokens, pieces, slots, first_rows):
    seq, width = tokens.shape
    smem = pl.BlockSpec(memory_space=pltpu.SMEM)
    vmem = pl.BlockSpec(memory_space=pltpu.VMEM)
    columns = pieces[0].shape[2]
    return pl.pallas_call(
        head_kernel,
        out_shape=[jax.ShapeDtypeStruct((seq // NX, width), jnp.bfloat16)] * NX,
        in_specs=[smem] * 2 + [vmem] * 5,
        out_specs=[vmem] * NX,
        scratch_shapes=[
            pltpu.VMEM((width, columns), jnp.bfloat16),
            pltpu.VMEM((seq, columns // 4), jnp.bfloat16),
        ],
        compiler_params=pltpu.CompilerParams(vmem_limit_bytes=40 * 1024 * 1024),
        cost_estimate=pl.CostEstimate(
            flops=2 * seq * width * columns,
            bytes_accessed=8 * seq * width,
            transcendentals=seq * seq,
        ),
    )(slots, first_rows, tokens, *pieces)


def sum_kernel(p0, p1, p2, p3, o_ref):
    step = 1024
    for c in range(0, o_ref.shape[1], step):
        here = slice(c, c + step)
        total = p0[:, here].astype(jnp.float32)
        for ref in (p1, p2, p3):
            total = total + ref[:, here].astype(jnp.float32)
        o_ref[:, here] = total.astype(o_ref.dtype)


def summed(blocks):
    rows, width = blocks[0].shape
    vmem = pl.BlockSpec(memory_space=pltpu.VMEM)
    return pl.pallas_call(
        sum_kernel,
        out_shape=jax.ShapeDtypeStruct((rows, width), jnp.bfloat16),
        in_specs=[vmem] * NX,
        out_specs=vmem,
        compiler_params=pltpu.CompilerParams(vmem_limit_bytes=16 * 1024 * 1024),
        cost_estimate=pl.CostEstimate(
            flops=4 * rows * width, bytes_accessed=10 * rows * width, transcendentals=0
        ),
    )(*blocks)


def mean_kernel(t_ref, parts_ref, latent_ref, stored_ref, table_ref, mean_ref, sum_ref):
    t = t_ref[0]
    dt = (t.astype(jnp.float32) + 1.0) / table_ref.shape[1]
    rows, width = latent_ref.shape
    step = 512
    squares = jnp.zeros((rows, step), jnp.float32)
    for c in range(0, width, step):
        here = slice(c, c + step)
        proj = parts_ref[0, :, here].astype(jnp.float32)
        for k in range(1, parts_ref.shape[0]):
            proj = proj + parts_ref[k, :, here].astype(jnp.float32)
        latent = latent_ref[:, here].astype(jnp.float32)
        mean = latent - dt * (latent + table_ref[2, pl.ds(t, 1), here] * proj)
        mean_ref[:, here] = mean.astype(jnp.bfloat16)
        residual = stored_ref[:, here].astype(jnp.float32) - mean
        squares = squares + residual * residual
    total = jnp.sum(squares, axis=(0, 1), keepdims=True)
    sum_ref[...] = jnp.broadcast_to(total[None], sum_ref.shape)


def mean_and_squares(t, parts, latent, stored, table):
    rows, width = latent.shape
    vmem = pl.BlockSpec(memory_space=pltpu.VMEM)
    return pl.pallas_call(
        mean_kernel,
        out_shape=(
            jax.ShapeDtypeStruct((rows, width), jnp.bfloat16),
            jax.ShapeDtypeStruct((NZL * NX, 1, 128), jnp.float32),
        ),
        in_specs=[pl.BlockSpec(memory_space=pltpu.SMEM)] + [vmem] * 4,
        out_specs=(vmem, vmem),
        compiler_params=pltpu.CompilerParams(vmem_limit_bytes=16 * 1024 * 1024),
        cost_estimate=pl.CostEstimate(
            flops=16 * rows * width, bytes_accessed=16 * rows * width, transcendentals=0
        ),
    )(t, parts, latent, stored, table)


def one_device(latents, stored_sample, timestep, owner_map, mod_table, qkv_weight, out_weight):
    _, tok_local, width = latents.shape
    seq_len = tok_local * NZL * NX
    table = jnp.swapaxes(mod_table, 0, 1)
    time_float = timestep[0].astype(jnp.float32)
    sigma = 0.3 + 0.1 * time_float
    spread = 2.0 * sigma * sigma * seq_len * width
    offset = jnp.log(sigma) + 0.5 * math.log(2.0 * math.pi)

    weights = jnp.concatenate([qkv_weight, out_weight.T], axis=1)
    plane = lax.all_gather(weights, "zh", tiled=False)
    sent, plane = lax.optimization_barrier((latents[0], plane))
    copies = normalised_copies(timestep, sent, table, NZL * NX)
    tokens = lax.all_to_all(copies, TENSOR, split_axis=0, concat_axis=0, tiled=True)
    near, far = around_y(plane)
    pieces = (near, far, swapped(near), swapped(far))

    ahead = (owner_map // (NZH * NCORE) - lax.axis_index("y")) % NY
    place = jnp.zeros_like(ahead)
    for distance, where in enumerate(PLACE):
        place = jnp.where(ahead == distance, where, place)
    side = (owner_map % NCORE != lax.axis_index("core")).astype(jnp.int32)
    at = (side * NY + place) * NZH + (owner_map // NCORE) % NZH
    slices = jnp.arange(at.shape[0], dtype=jnp.int32)
    slots = jnp.sum(jnp.where(at[None, :] == slices[:, None], slices[None, :], 0), axis=1)

    turn = jnp.arange(NX * NZL, dtype=jnp.int32)
    to_x = (lax.axis_index("x") + turn // NZL) % NX
    first_rows = ((turn % NZL * NX + to_x) * tok_local).astype(jnp.int32)

    terms = head_term(tokens.reshape(seq_len, width), pieces, slots, first_rows)
    by_x = [terms[0]] + [
        lax.ppermute(terms[r], "x", [(i, (i + r) % NX) for i in range(NX)]) for r in (2, 1, 3)
    ]
    some, latent, stored, table, spread, offset = lax.optimization_barrier(
        (summed(by_x), latents[0], stored_sample[0], table, spread, offset)
    )
    parts = lax.all_to_all(
        some.reshape(NZL, tok_local, width), "zl", split_axis=0, concat_axis=0, tiled=True
    )
    mean, squares = mean_and_squares(timestep, parts, latent, stored, table)
    mean, squares, spread, offset = lax.optimization_barrier((mean, squares, spread, offset))
    squares = lax.all_to_all(squares, TENSOR, split_axis=0, concat_axis=0, tiled=True)
    log_prob = -jnp.sum(squares[:, :, :1]) / spread - offset
    return (mean[None], log_prob[None])


def solution(mesh):
    fine = Mesh(mesh.devices.reshape(NY, NZH, NCORE, NZL, NX), GROUP + TENSOR)
    in_specs = (
        P(GROUP, TENSOR, None),
        P(GROUP, TENSOR, None),
        P(GROUP),
        P(),
        P(),
        P(GROUP, TENSOR),
        P(TENSOR, GROUP),
    )
    out_specs = (P(GROUP, TENSOR, None), P(GROUP))
    return jax.shard_map(one_device, mesh=fine, in_specs=in_specs, out_specs=out_specs, check_vma=False)
```

```python
import math

import jax
import jax.numpy as jnp
from jax import lax
from jax.experimental import pallas as pl
from jax.experimental.pallas import tpu as pltpu
from jax.sharding import Mesh, PartitionSpec as P


GROUP = ("y", "zh", "core")
TENSOR = ("zl", "x")
NY, NZH, NCORE, NZL, NX = 8, 4, 2, 4, 4
NT = (((1,), (1,)), ((), ()))


def shifted(x, by):
    return lax.ppermute(x, "y", [(i, (i + by) % NY) for i in range(NY)])


def swapped(x):
    return lax.ppermute(x, "core", [(0, 1), (1, 0)])


PLACE = (0, 2, 6, 5, 3, 7, 4, 1)


def around_y(x):
    below = shifted(x, 1)
    above = shifted(x, -1)
    across = shifted(x, 4)
    near = jnp.concatenate([x, below, above, across], axis=0)
    up = shifted(jnp.concatenate([below, across], axis=0), 1)
    down = shifted(jnp.concatenate([above, across], axis=0), -1)
    return near, jnp.concatenate([up, down], axis=0)


def norm_kernel(x_ref, rows_ref, o_ref):
    x = x_ref[...].astype(jnp.float32)
    width = x.shape[1]
    centred = x - jnp.sum(x, axis=1, keepdims=True) / width
    variance = jnp.sum(centred * centred, axis=1, keepdims=True) / width
    normed = centred * lax.rsqrt(variance + 1e-06)
    modulated = (normed * (1.0 + rows_ref[1:2, :]) + rows_ref[0:1, :]).astype(jnp.bfloat16)
    for i in range(o_ref.shape[0]):
        o_ref[i] = modulated


def normalised_copies(tokens, mod, copies):
    rows, width = tokens.shape
    vmem = pl.BlockSpec(memory_space=pltpu.VMEM)
    return pl.pallas_call(
        norm_kernel,
        out_shape=jax.ShapeDtypeStruct((copies, rows, width), jnp.bfloat16),
        in_specs=[vmem, vmem],
        out_specs=vmem,
        compiler_params=pltpu.CompilerParams(vmem_limit_bytes=16 * 1024 * 1024),
        cost_estimate=pl.CostEstimate(
            flops=12 * rows * width, bytes_accessed=40 * rows * width, transcendentals=rows
        ),
    )(tokens, mod)


def head_kernel(to_ref, row_ref, x_ref, own0, own1, other0, other1, *rest):
    outs, (w_ref, a_ref) = rest[:NX], rest[NX:]
    count, rows, columns = own0.shape
    width = x_ref.shape[1]
    hd = columns // 4
    for part, ref in enumerate((own0, own1, other0, other1)):
        for k in range(count):
            first = pl.multiple_of(to_ref[part * count + k] * rows, rows)
            w_ref[pl.ds(first, rows), :] = ref[k]

    qkv = jnp.dot(x_ref[...], w_ref[:, : 3 * hd], preferred_element_type=jnp.float32)
    qkv = qkv.astype(jnp.bfloat16)
    q, k, v = qkv[:, :hd], qkv[:, hd : 2 * hd], qkv[:, 2 * hd :]
    scores = lax.dot_general(q, k, NT, preferred_element_type=jnp.float32) / math.sqrt(hd)
    expo = jnp.exp(scores - jnp.max(scores, axis=1, keepdims=True))
    probs = (expo / jnp.sum(expo, axis=1, keepdims=True)).astype(jnp.bfloat16)
    attended = jnp.dot(probs, v, preferred_element_type=jnp.float32)
    a_ref[...] = attended.astype(jnp.bfloat16)
    blocks = row_ref.shape[0]
    tok = a_ref.shape[0] // blocks
    ordered = jnp.concatenate(
        [a_ref[pl.ds(pl.multiple_of(row_ref[i], tok), tok), :] for i in range(blocks)], axis=0
    )
    step = 512
    part = ordered.shape[0] // NX
    for c in range(0, width, step):
        w_out = w_ref[c : c + step, 3 * hd :]
        term = lax.dot_general(ordered, w_out, NT, preferred_element_type=jnp.float32)
        term = term.astype(jnp.bfloat16)
        for r, o_ref in enumerate(outs):
            o_ref[:, c : c + step] = term[r * part : (r + 1) * part]


def head_term(tokens, pieces, slots, first_rows):
    seq, width = tokens.shape
    smem = pl.BlockSpec(memory_space=pltpu.SMEM)
    vmem = pl.BlockSpec(memory_space=pltpu.VMEM)
    columns = pieces[0].shape[2]
    return pl.pallas_call(
        head_kernel,
        out_shape=[jax.ShapeDtypeStruct((seq // NX, width), jnp.bfloat16)] * NX,
        in_specs=[smem] * 2 + [vmem] * 5,
        out_specs=[vmem] * NX,
        scratch_shapes=[
            pltpu.VMEM((width, columns), jnp.bfloat16),
            pltpu.VMEM((seq, columns // 4), jnp.bfloat16),
        ],
        compiler_params=pltpu.CompilerParams(vmem_limit_bytes=40 * 1024 * 1024),
        cost_estimate=pl.CostEstimate(
            flops=2 * seq * width * columns,
            bytes_accessed=8 * seq * width,
            transcendentals=seq * seq,
        ),
    )(slots, first_rows, tokens, *pieces)


def sum_kernel(p0, p1, p2, p3, o_ref):
    step = 1024
    for c in range(0, o_ref.shape[1], step):
        here = slice(c, c + step)
        total = p0[:, here].astype(jnp.float32)
        for ref in (p1, p2, p3):
            total = total + ref[:, here].astype(jnp.float32)
        o_ref[:, here] = total.astype(o_ref.dtype)


def summed(blocks):
    rows, width = blocks[0].shape
    vmem = pl.BlockSpec(memory_space=pltpu.VMEM)
    return pl.pallas_call(
        sum_kernel,
        out_shape=jax.ShapeDtypeStruct((rows, width), jnp.bfloat16),
        in_specs=[vmem] * NX,
        out_specs=vmem,
        compiler_params=pltpu.CompilerParams(vmem_limit_bytes=16 * 1024 * 1024),
        cost_estimate=pl.CostEstimate(
            flops=4 * rows * width, bytes_accessed=10 * rows * width, transcendentals=0
        ),
    )(*blocks)


def mean_kernel(t_ref, parts_ref, latent_ref, stored_ref, table_ref, mean_ref, sum_ref):
    t = t_ref[0]
    dt = (t.astype(jnp.float32) + 1.0) / table_ref.shape[1]
    rows, width = latent_ref.shape
    step = 512
    squares = jnp.zeros((rows, step), jnp.float32)
    for c in range(0, width, step):
        here = slice(c, c + step)
        proj = parts_ref[0, :, here].astype(jnp.float32)
        for k in range(1, parts_ref.shape[0]):
            proj = proj + parts_ref[k, :, here].astype(jnp.float32)
        latent = latent_ref[:, here].astype(jnp.float32)
        mean = latent - dt * (latent + table_ref[2, pl.ds(t, 1), here] * proj)
        mean_ref[:, here] = mean.astype(jnp.bfloat16)
        residual = stored_ref[:, here].astype(jnp.float32) - mean
        squares = squares + residual * residual
    total = jnp.sum(squares, axis=(0, 1), keepdims=True)
    sum_ref[...] = jnp.broadcast_to(total[None], sum_ref.shape)


def mean_and_squares(t, parts, latent, stored, table):
    rows, width = latent.shape
    vmem = pl.BlockSpec(memory_space=pltpu.VMEM)
    return pl.pallas_call(
        mean_kernel,
        out_shape=(
            jax.ShapeDtypeStruct((rows, width), jnp.bfloat16),
            jax.ShapeDtypeStruct((NZL * NX, 1, 128), jnp.float32),
        ),
        in_specs=[pl.BlockSpec(memory_space=pltpu.SMEM)] + [vmem] * 4,
        out_specs=(vmem, vmem),
        compiler_params=pltpu.CompilerParams(vmem_limit_bytes=16 * 1024 * 1024),
        cost_estimate=pl.CostEstimate(
            flops=16 * rows * width, bytes_accessed=16 * rows * width, transcendentals=0
        ),
    )(t, parts, latent, stored, table)


def one_device(latents, stored_sample, timestep, owner_map, mod_table, qkv_weight, out_weight):
    _, tok_local, width = latents.shape
    seq_len = tok_local * NZL * NX
    table = jnp.swapaxes(mod_table, 0, 1)
    time_float = timestep[0].astype(jnp.float32)
    sigma = 0.3 + 0.1 * time_float
    spread = 2.0 * sigma * sigma * seq_len * width
    offset = jnp.log(sigma) + 0.5 * math.log(2.0 * math.pi)

    mod = lax.dynamic_index_in_dim(mod_table, timestep[0], 0, keepdims=False)
    weights = jnp.concatenate([qkv_weight, out_weight.T], axis=1)
    plane = lax.all_gather(weights, "zh", tiled=False)
    copies = normalised_copies(latents[0], mod, NZL * NX)
    tokens = lax.all_to_all(copies, TENSOR, split_axis=0, concat_axis=0, tiled=True)
    near, far = around_y(plane)
    pieces = (near, far, swapped(near), swapped(far))

    ahead = (owner_map // (NZH * NCORE) - lax.axis_index("y")) % NY
    place = jnp.zeros_like(ahead)
    for distance, where in enumerate(PLACE):
        place = jnp.where(ahead == distance, where, place)
    side = (owner_map % NCORE != lax.axis_index("core")).astype(jnp.int32)
    at = (side * NY + place) * NZH + (owner_map // NCORE) % NZH
    slices = jnp.arange(at.shape[0], dtype=jnp.int32)
    slots = jnp.sum(jnp.where(at[None, :] == slices[:, None], slices[None, :], 0), axis=1)

    turn = jnp.arange(NX * NZL, dtype=jnp.int32)
    to_x = (lax.axis_index("x") + turn // NZL) % NX
    first_rows = ((turn % NZL * NX + to_x) * tok_local).astype(jnp.int32)

    terms = head_term(tokens.reshape(seq_len, width), pieces, slots, first_rows)
    by_x = [terms[0]] + [
        lax.ppermute(terms[r], "x", [(i, (i + r) % NX) for i in range(NX)]) for r in (2, 1, 3)
    ]
    some, latent, stored, table, spread, offset = lax.optimization_barrier(
        (summed(by_x), latents[0], stored_sample[0], table, spread, offset)
    )
    parts = lax.all_to_all(
        some.reshape(NZL, tok_local, width), "zl", split_axis=0, concat_axis=0, tiled=True
    )
    mean, squares = mean_and_squares(timestep, parts, latent, stored, table)
    mean, squares, spread, offset = lax.optimization_barrier((mean, squares, spread, offset))
    squares = lax.all_to_all(squares, TENSOR, split_axis=0, concat_axis=0, tiled=True)
    log_prob = -jnp.sum(squares[:, :, :1]) / spread - offset
    return (mean[None], log_prob[None])


def solution(mesh):
    fine = Mesh(mesh.devices.reshape(NY, NZH, NCORE, NZL, NX), GROUP + TENSOR)
    in_specs = (
        P(GROUP, TENSOR, None),
        P(GROUP, TENSOR, None),
        P(GROUP),
        P(),
        P(),
        P(GROUP, TENSOR),
        P(TENSOR, GROUP),
    )
    out_specs = (P(GROUP, TENSOR, None), P(GROUP))
    return jax.shard_map(one_device, mesh=fine, in_specs=in_specs, out_specs=out_specs, check_vma=False)
```
